32 devices in a mesh: dp: 4 (over z), fsdp: 8 (over y, x, core).
Axes of the slice: x: 2, y: 2, z: 4, core: 2. Of those that a mesh axis runs over, the one named last changes fastest.
Arguments:
- images: bfloat16 [2, 64, 197, 384], P(None, ('dp', 'fsdp')), may hold values from -6 to 6
- cotangent: float32 [2, 64, 197, 384], P(None, ('dp', 'fsdp')), may hold values from -6 to 6
- image_counts: int32 [2, 32], P(None, ('dp', 'fsdp')), may hold values from 0 to 2, as said below
- ln1_gain: bfloat16 [384], P('fsdp'), may hold values from 0.5 to 1.5
- ln1_bias: bfloat16 [384], P('fsdp'), may hold values from -3 to 3
- qkv_weight: bfloat16 [384, 1152], P('fsdp'), may hold values from -1 to 1
- q_bias: bfloat16 [384], P('fsdp'), may hold values from -3 to 3
- v_bias: bfloat16 [384], P('fsdp'), may hold values from -3 to 3
- out_weight: bfloat16 [384, 384], P('fsdp'), may hold values from -1.5 to 1.5
- out_bias: bfloat16 [384], P('fsdp'), may hold values from -3 to 3
- ln2_gain: bfloat16 [384], P('fsdp'), may hold values from 0.5 to 1.5
- ln2_bias: bfloat16 [384], P('fsdp'), may hold values from -3 to 3
- fc1_weight: bfloat16 [384, 1536], P('fsdp'), may hold values from -0.3125 to 0.3125
- fc1_bias: bfloat16 [1536], P('fsdp'), may hold values from -3 to 3
- fc2_weight: bfloat16 [1536, 384], P('fsdp'), may hold values from -0.15625 to 0.15625
- fc2_bias: bfloat16 [384], P('fsdp'), may hold values from -3 to 3
Outputs:
- block_out: bfloat16 [2, 64, 197, 384], P(None, ('dp', 'fsdp'))
- image_grad: float32 [2, 64, 197, 384], P(None, ('dp', 'fsdp'))
- ln1_gain_grad: float32 [384], P('fsdp')
- ln1_bias_grad: float32 [384], P('fsdp')
- qkv_weight_grad: float32 [384, 1152], P('fsdp')
- q_bias_grad: float32 [384], P('fsdp')
- v_bias_grad: float32 [384], P('fsdp')
- out_weight_grad: float32 [384, 384], P('fsdp')
- out_bias_grad: float32 [384], P('fsdp')
- ln2_gain_grad: float32 [384], P('fsdp')
- ln2_bias_grad: float32 [384], P('fsdp')
- fc1_weight_grad: float32 [384, 1536], P('fsdp')
- fc1_bias_grad: float32 [1536], P('fsdp')
- fc2_weight_grad: float32 [1536, 384], P('fsdp')
- fc2_bias_grad: float32 [384], P('fsdp')
The draws below stay inside these ranges and needn't reach their ends.
Inputs may be any that keep to these rules, and one draw needn't show every extreme that they name: `image_counts`: in every micro-batch some device has all 2 slots live; slots at or past a device's count are empty.
All inputs are finite; a program needn't handle non-finite values.
Results may differ from the reference program's by a relative error of at most 0.013.
The reference program's roundings to bfloat16 on the way count: a program that leaves them out, or rounds other values in their place, can miss the bound.
Values may be sent and summed in bfloat16 or wider, within the bound.
A program may use at most 128 MiB of HBM per device.

```python
import jax
import jax.numpy as jnp
from jax import lax

D = 384
H = 6
HD = 64
FF = 1536
S = 197
SLOTS = 2
MB = 2
IMAGES = 64
N_DP = 4
N_FSDP = 8


def draw_image_counts(key, part):
    first, second = jax.random.split(jax.random.fold_in(key, 17))
    devices_all = N_DP * N_FSDP
    counts = jax.random.randint(first, (MB, devices_all), 0, SLOTS + 1)
    spots = jax.random.randint(second, (MB,), 0, devices_all)
    full = jnp.arange(devices_all)[None, :] == spots[:, None]
    return jnp.where(full, SLOTS, counts).astype(jnp.int32)


def draw_qkv_weight(key, part):
    noise = jnp.clip(jax.random.normal(jax.random.fold_in(key, 7), (D, 3 * D), jnp.float32), -6.0, 6.0) * D ** (-0.5)
    return jnp.clip(noise, -1.0, 1.0).astype(jnp.bfloat16)


def draw_images(key, part):
    noise = jnp.clip(jax.random.normal(jax.random.fold_in(key, 11), (MB, IMAGES, S, D), jnp.float32), -6.0, 6.0)
    return noise.astype(jnp.bfloat16)


def raised(entries, stream_key, source, target, blocks, factor):
    def block_of(axis_at):
        return (jnp.arange(entries.shape[axis_at]) // (entries.shape[axis_at] // blocks)).reshape((-1,) + (1,) * (entries.ndim - 1 - axis_at))

    near = jax.random.permutation(stream_key, blocks)[block_of(target)]
    second = (block_of(target) + blocks // 2) % blocks
    return jnp.where((block_of(source) == near) | (block_of(source) == second), factor * entries, entries)


def levels(own_key, extent, pieces, smallest, largest):
    def one(axis_at, blocks):
        heights = jax.random.uniform(jax.random.fold_in(jax.random.fold_in(own_key, 6), axis_at), (blocks,), jnp.float32, smallest / len(pieces), largest / len(pieces))
        return jnp.repeat(jnp.exp(heights), extent[axis_at] // blocks).reshape((-1,) + (1,) * (len(extent) - axis_at - 1))

    gain = one(*pieces[0])
    for cut in pieces[1:]:
        gain = gain * one(*cut)
    return gain


def bell_draw(own_key, shape, scale, bound, shards=(), dtype=jnp.bfloat16):
    drawn = jax.random.normal(own_key, shape, jnp.float32) * scale
    if len(shards) > 0:
        drawn = levels(own_key, shape, shards, -0.22, 0.18) * drawn
    return jnp.clip(drawn, min=-bound, max=bound).astype(dtype)


def gaussian_with(stream_key, dims, scale, bound, pieces, heavy, dtype=jnp.bfloat16):
    drawn = scale * jax.random.normal(stream_key, dims, jnp.float32)
    if pieces:
        drawn = drawn * levels(stream_key, dims, pieces, -0.22, 0.18)
    return jnp.clip(raised(drawn, jax.random.fold_in(stream_key, 3), *heavy), -bound, bound).astype(dtype)


def setup_inputs(seed: int = 0) -> dict:
    key_of = jax.random.split(jax.random.key(seed), 17)
    images = draw_images(jax.random.fold_in(key_of[16], 71), 0)
    cotangent = gaussian_with(key_of[1], (MB, IMAGES, S, D), 1.0, 6.0, ((1, 32),), (1, 3, 32, 2.75), jnp.float32)
    image_counts = draw_image_counts(jax.random.fold_in(key_of[16], 71), 0)
    ln1_gain = jnp.clip(1.0 + 0.1 * jax.random.normal(key_of[3], (D,), jnp.float32), 0.5, 1.5).astype(jnp.bfloat16)
    ln1_bias = bell_draw(key_of[4], (D,), 0.5, 3.0, ((0, 8),))
    qkv_weight = draw_qkv_weight(jax.random.fold_in(key_of[16], 71), 0)
    q_bias = bell_draw(key_of[6], (D,), 0.5, 3.0, ((0, 8),))
    v_bias = bell_draw(key_of[7], (D,), 0.5, 3.0, ((0, 8),))
    out_weight = bell_draw(key_of[8], (D, D), (D // 24) ** -0.5, 1.5, ((0, 8),))
    out_bias = bell_draw(key_of[9], (D,), 0.5, 3.0, ((0, 8),))
    ln2_gain = jnp.clip(1.0 + 0.1 * jax.random.normal(key_of[10], (D,), jnp.float32), 0.5, 1.5).astype(jnp.bfloat16)
    ln2_bias = bell_draw(key_of[11], (D,), 0.5, 3.0, ((0, 8),))
    fc1_weight = bell_draw(key_of[12], (D, FF), D ** -0.5, 0.3125, ((0, 8),))
    fc1_bias = bell_draw(key_of[13], (FF,), 0.5, 3.0, ((0, 8),))
    fc2_weight = bell_draw(key_of[14], (FF, D), FF ** -0.5, 0.15625, ((0, 8),))
    fc2_bias = bell_draw(key_of[15], (D,), 0.5, 3.0, ((0, 8),))
    return dict(images=images, cotangent=cotangent, image_counts=image_counts, ln1_gain=ln1_gain, ln1_bias=ln1_bias, qkv_weight=qkv_weight, q_bias=q_bias, v_bias=v_bias, out_weight=out_weight, out_bias=out_bias, ln2_gain=ln2_gain, ln2_bias=ln2_bias, fc1_weight=fc1_weight, fc1_bias=fc1_bias, fc2_weight=fc2_weight, fc2_bias=fc2_bias)


def product(form, left, right):
    return jnp.einsum(form, left.astype(jnp.float32), right.astype(jnp.float32))

def layer_norm(hidden):
    center = hidden - lax.optimization_barrier(jnp.mean(hidden, axis=-1, keepdims=True))
    rstd = lax.rsqrt(lax.optimization_barrier(jnp.mean(center * center, axis=-1, keepdims=True)) + 1e-06)
    return (center * rstd, rstd)

def norm_back(grad, normed, rstd):
    return rstd * (grad - lax.optimization_barrier(jnp.mean(grad, axis=-1, keepdims=True)) - normed * lax.optimization_barrier(jnp.mean(grad * normed, axis=-1, keepdims=True)))

def normal_cdf(value):
    return 0.5 * (1.0 + lax.erf(value * 0.7071067811865476))

def gelu_slope(value):
    return normal_cdf(value) + value * jnp.exp(-0.5 * value * value) * 0.3989422804014327

def heads(tensor):
    return tensor.reshape(tensor.shape[0], tensor.shape[1], H, HD)

def run_forward(images, weights):
    gain_one, bias_one, w_qkv, bias_q, bias_v, w_out, bias_out, gain_two, bias_two, w_fc1, bias_fc1, w_fc2, bias_fc2 = weights
    width = w_qkv.shape[0]
    scale = HD ** (-0.5)
    hidden = images.astype(jnp.float32)
    normed1, rstd1 = layer_norm(hidden)
    attn_in = (normed1 * gain_one.astype(jnp.float32) + bias_one.astype(jnp.float32)).astype(jnp.bfloat16)
    mixed = product('bsd,de->bse', attn_in, w_qkv)
    query = ((mixed[..., :width] + bias_q.astype(jnp.float32)) * scale).astype(jnp.bfloat16)
    keys = mixed[..., width:2 * width].astype(jnp.bfloat16)
    values = (mixed[..., 2 * width:] + bias_v.astype(jnp.float32)).astype(jnp.bfloat16)
    scores = product('bqhe,bkhe->bhqk', heads(query), heads(keys))
    top = lax.optimization_barrier(jnp.max(scores, axis=-1, keepdims=True))
    expo = jnp.exp(scores - top)
    total = lax.optimization_barrier(jnp.sum(expo, axis=-1, keepdims=True))
    probs = expo / total
    lse = top + jnp.log(total)
    attn = product('bhqk,bkhe->bqhe', probs.astype(jnp.bfloat16), heads(values))
    attn = attn.reshape(hidden.shape).astype(jnp.bfloat16)
    resid = hidden + product('bsd,de->bse', attn, w_out) + bias_out.astype(jnp.float32)
    normed2, rstd2 = layer_norm(resid)
    mlp_in = (normed2 * gain_two.astype(jnp.float32) + bias_two.astype(jnp.float32)).astype(jnp.bfloat16)
    pre = product('bsd,df->bsf', mlp_in, w_fc1) + bias_fc1.astype(jnp.float32)
    act = (pre * normal_cdf(pre)).astype(jnp.bfloat16)
    result = resid + product('bsf,fd->bsd', act, w_fc2) + bias_fc2.astype(jnp.float32)
    saved = (normed1, rstd1, attn_in, query, keys, values, lse, attn, normed2, rstd2, mlp_in, pre, act)
    return (result, saved)

def run_backward(cot, saved, weights):
    gain_one, bias_one, w_qkv, bias_q, bias_v, w_out, bias_out, gain_two, bias_two, w_fc1, bias_fc1, w_fc2, bias_fc2 = weights
    normed1, rstd1, attn_in, query, keys, values, lse, attn, normed2, rstd2, mlp_in, pre, act = saved
    scale = HD ** (-0.5)
    rows = (0, 1)
    grad_b = cot.astype(jnp.bfloat16)
    grad_fc2 = product('bsf,bsd->fd', act, grad_b)
    grad_bias_fc2 = lax.optimization_barrier(jnp.sum(cot, axis=rows))
    d_pre = product('bsd,fd->bsf', grad_b, w_fc2) * gelu_slope(pre)
    d_pre_b = d_pre.astype(jnp.bfloat16)
    grad_fc1 = product('bsd,bsf->df', mlp_in, d_pre_b)
    grad_bias_fc1 = lax.optimization_barrier(jnp.sum(d_pre, axis=rows))
    d_mlp = product('bsf,df->bsd', d_pre_b, w_fc1)
    grad_gain_two = lax.optimization_barrier(jnp.sum(d_mlp * normed2, axis=rows))
    grad_bias_two = lax.optimization_barrier(jnp.sum(d_mlp, axis=rows))
    d_resid = cot + norm_back(d_mlp * gain_two.astype(jnp.float32), normed2, rstd2)
    d_proj = d_resid.astype(jnp.bfloat16)
    grad_out = product('bsd,bse->de', attn, d_proj)
    grad_bias_out = lax.optimization_barrier(jnp.sum(d_resid, axis=rows))
    d_attn = product('bse,de->bsd', d_proj, w_out).astype(jnp.bfloat16)
    scores = product('bqhe,bkhe->bhqk', heads(query), heads(keys))
    probs = jnp.exp(scores - lse)
    d_values = product('bhqk,bqhe->bkhe', probs.astype(jnp.bfloat16), heads(d_attn))
    d_probs = product('bqhe,bkhe->bhqk', heads(d_attn), heads(values))
    delta = lax.optimization_barrier(jnp.sum(probs * d_probs, axis=-1, keepdims=True))
    d_scores = (probs * (d_probs - delta)).astype(jnp.bfloat16)
    d_query = product('bhqk,bkhe->bqhe', d_scores, heads(keys)) * scale
    d_keys = product('bhqk,bqhe->bkhe', d_scores, heads(query))
    shape = d_resid.shape
    d_query = d_query.reshape(shape)
    d_keys = d_keys.reshape(shape)
    d_values = d_values.reshape(shape)
    d_mixed = jnp.concatenate([d_query, d_keys, d_values], axis=-1).astype(jnp.bfloat16)
    grad_qkv = product('bsd,bse->de', attn_in, d_mixed)
    grad_bias_q = lax.optimization_barrier(jnp.sum(d_query, axis=rows))
    grad_bias_v = lax.optimization_barrier(jnp.sum(d_values, axis=rows))
    d_in = product('bse,de->bsd', d_mixed, w_qkv)
    grad_gain_one = lax.optimization_barrier(jnp.sum(d_in * normed1, axis=rows))
    grad_bias_one = lax.optimization_barrier(jnp.sum(d_in, axis=rows))
    d_images = d_resid + norm_back(d_in * gain_one.astype(jnp.float32), normed1, rstd1)
    grads = (grad_gain_one, grad_bias_one, grad_qkv, grad_bias_q, grad_bias_v, grad_out, grad_bias_out, grad_gain_two, grad_bias_two, grad_fc1, grad_bias_fc1, grad_fc2, grad_bias_fc2)
    return (d_images, grads)

def reference(images, cotangent, image_counts, ln1_gain, ln1_bias, qkv_weight, q_bias, v_bias, out_weight, out_bias, ln2_gain, ln2_bias, fc1_weight, fc1_bias, fc2_weight, fc2_bias):
    weights = (ln1_gain, ln1_bias, qkv_weight, q_bias, v_bias, out_weight, out_bias, ln2_gain, ln2_bias, fc1_weight, fc1_bias, fc2_weight, fc2_bias)
    micro, total, seq, width = images.shape
    group = SLOTS * 4
    blocks = total // group
    index = jnp.arange(total).astype(jnp.int32)
    owner = index // SLOTS
    slot_of = index % SLOTS
    live = (slot_of[None, :] < image_counts[:, owner]).astype(jnp.float32)
    masked = cotangent * live[:, :, None, None]
    image_blocks = images.reshape(micro * blocks, group, seq, width)
    cot_blocks = masked.reshape(micro * blocks, group, seq, width)
    live_blocks = live.reshape(micro * blocks, group)

    def step(carry, item):
        block, cot, alive = item
        result, saved = run_forward(block, weights)
        d_images, grads = run_backward(cot, saved, weights)
        carry = jax.tree.map(lambda acc, new: acc + new, carry, grads)
        return (carry, ((result * alive[:, None, None]).astype(jnp.bfloat16), d_images))
    start = tuple((jnp.zeros(w.shape, jnp.float32) for w in weights))
    grads, (outs, d_outs) = lax.scan(step, start, (image_blocks, cot_blocks, live_blocks))
    block_out = outs.reshape(micro, total, seq, width)
    image_grad = d_outs.reshape(micro, total, seq, width)
    return (block_out, image_grad, grads[0], grads[1], grads[2], grads[3], grads[4], grads[5], grads[6], grads[7], grads[8], grads[9], grads[10], grads[11], grads[12])
```

```python
import functools

import jax
import jax.numpy as jnp
from jax import lax
from jax.experimental import pallas as pl
from jax.experimental.pallas import tpu as pltpu
from jax.sharding import PartitionSpec as P

H = 6
HD = 64
LANE = 128
BLOCKS = 8
SMALL = 16


def dot(left, right, left_dim, right_dim):
    return lax.dot_general(
        left,
        right,
        (((left_dim,), (right_dim,)), ((), ())),
        preferred_element_type=jnp.float32,
    )


def layer_norm(hidden):
    center = hidden - jnp.mean(hidden, axis=-1, keepdims=True)
    rstd = lax.rsqrt(jnp.mean(center * center, axis=-1, keepdims=True) + 1e-06)
    return (center * rstd, rstd)


def norm_back(grad, normed, rstd):
    return rstd * (
        grad
        - jnp.mean(grad, axis=-1, keepdims=True)
        - normed * jnp.mean(grad * normed, axis=-1, keepdims=True)
    )


def block_kernel(
    last, tokens, alive_ref, img_ref, cot_ref, w_ref, out_ref, dimg_ref, g_ref,
    hid, cot, acc, sacc, probs_s, q_s, k_s, v_s, attn_s,
):
    step = pl.program_id(0)
    width = hid.shape[1]
    rows = hid.shape[0]
    part = width // BLOCKS
    ff_parts = (w_ref.shape[1] - SMALL - 4 * part) // (2 * part)
    bf16 = jnp.bfloat16
    f32 = jnp.float32

    @pl.when(step == 0)
    def _():
        hid[...] = jnp.zeros_like(hid)
        cot[...] = jnp.zeros_like(cot)
        acc[...] = jnp.zeros_like(acc)
        sacc[...] = jnp.zeros_like(sacc)

    alive = alive_ref[step]
    hid[0:tokens, :] = img_ref[0].astype(f32)
    cot[0:tokens, :] = cot_ref[0] * alive

    small = jnp.sum(w_ref[:, w_ref.shape[1] - SMALL :, :].astype(f32), axis=0)

    def vec(index):
        return small[index : index + 1, :]

    def weight(index):
        return w_ref[:, index * part : (index + 1) * part, :].reshape(width, width)

    def add(index, value):
        acc[:, index * part : (index + 1) * part, :] += value.reshape(BLOCKS, part, width)

    def fc2(index):
        start = (4 + ff_parts) * part
        chunk = BLOCKS // ff_parts
        return w_ref[index * chunk : (index + 1) * chunk, start : start + ff_parts * part, :].reshape(width, width)

    def add_fc2(index, value):
        start = (4 + ff_parts) * part
        chunk = BLOCKS // ff_parts
        acc[index * chunk : (index + 1) * chunk, start : start + ff_parts * part, :] += value.reshape(
            chunk, ff_parts * part, width
        )

    def add_small(index, value):
        sacc[index : index + 1, :] += jnp.sum(value, axis=0, keepdims=True)

    scale = HD ** (-0.5)
    normed1, rstd1 = layer_norm(hid[...])
    attn_in = (normed1 * vec(0) + vec(1)).astype(bf16)
    q_s[...] = ((dot(attn_in, weight(0), 1, 0) + vec(2)) * scale).astype(bf16)
    k_s[...] = dot(attn_in, weight(1), 1, 0).astype(bf16)
    v_s[...] = (dot(attn_in, weight(2), 1, 0) + vec(3)).astype(bf16)

    low = lax.broadcasted_iota(jnp.int32, (1, LANE), 1) < HD
    masks = (low.astype(f32).astype(bf16), (1.0 - low.astype(f32)).astype(bf16))
    keymask = lax.broadcasted_iota(jnp.int32, (rows, rows), 1) < tokens
    for pair in range(H // 2):
        cols = slice(pair * LANE, (pair + 1) * LANE)
        q, k, v = q_s[:, cols], k_s[:, cols], v_s[:, cols]
        halves = []
        for side in range(2):
            scores = jnp.where(keymask, dot(q * masks[side], k, 1, 1), -1e30)
            expo = jnp.exp(scores - jnp.max(scores, axis=-1, keepdims=True))
            probs = expo * (1.0 / jnp.sum(expo, axis=-1, keepdims=True))
            probs_s[2 * pair + side] = probs
            halves.append(dot(probs.astype(bf16), v, 1, 0))
        attn_s[:, cols] = jnp.where(low, halves[0], halves[1]).astype(bf16)

    attn = attn_s[...]
    resid = hid[...] + dot(attn, weight(3), 1, 0) + vec(4)
    normed2, rstd2 = layer_norm(resid)
    mlp_in = (normed2 * vec(5) + vec(6)).astype(bf16)
    grad_top = cot[...]
    dy = grad_top.astype(bf16)
    add_small(7, grad_top)
    result = resid + vec(7)
    d_mlp = jnp.zeros_like(resid)
    for index in range(ff_parts):
        w_one = weight(4 + index)
        w_two = fc2(index)
        pre = dot(mlp_in, w_one, 1, 0) + vec(8 + index)
        cdf = 0.5 * (1.0 + lax.erf(pre * 0.7071067811865476))
        slope = cdf + pre * jnp.exp(-0.5 * pre * pre) * 0.3989422804014327
        act = (pre * cdf).astype(bf16)
        result = result + dot(act, w_two, 1, 0)
        add_fc2(index, dot(act, dy, 0, 0))
        d_pre = dot(dy, w_two, 1, 1) * slope
        d_pre_b = d_pre.astype(bf16)
        add_small(8 + index, d_pre)
        add(4 + index, dot(mlp_in, d_pre_b, 0, 0))
        d_mlp = d_mlp + dot(d_pre_b, w_one, 1, 1)
    out_ref[0] = (result * alive)[0:tokens, :].astype(bf16)

    add_small(5, d_mlp * normed2)
    add_small(6, d_mlp)
    d_resid = grad_top + norm_back(d_mlp * vec(5), normed2, rstd2)
    d_proj = d_resid.astype(bf16)
    add(3, dot(attn, d_proj, 0, 0))
    add_small(4, d_resid)
    attn_s[...] = dot(d_proj, weight(3), 1, 1).astype(bf16)
    for pair in range(H // 2):
        cols = slice(pair * LANE, (pair + 1) * LANE)
        q, k, v, d_attn = q_s[:, cols], k_s[:, cols], v_s[:, cols], attn_s[:, cols]
        d_q, d_k, d_v = [], [], []
        for side in range(2):
            probs = probs_s[2 * pair + side]
            d_v.append(dot(probs.astype(bf16), d_attn, 0, 0))
            d_probs = dot(d_attn * masks[side], v, 1, 1)
            delta = jnp.sum(probs * d_probs, axis=-1, keepdims=True)
            d_scores = (probs * (d_probs - delta)).astype(bf16)
            d_q.append(dot(d_scores, k, 1, 0))
            d_k.append(dot(d_scores, q, 0, 0))
        d_query = jnp.where(low, d_q[0], d_q[1]) * scale
        d_values = jnp.where(low, d_v[0], d_v[1])
        sacc[2:3, cols] += jnp.sum(d_query, axis=0, keepdims=True)
        sacc[3:4, cols] += jnp.sum(d_values, axis=0, keepdims=True)
        q_s[:, cols] = d_query.astype(bf16)
        k_s[:, cols] = jnp.where(low, d_k[0], d_k[1]).astype(bf16)
        v_s[:, cols] = d_values.astype(bf16)
    d_in = jnp.zeros_like(d_resid)
    for index, piece in enumerate((q_s, k_s, v_s)):
        d_mixed = piece[...]
        add(index, dot(attn_in, d_mixed, 0, 0))
        d_in = d_in + dot(d_mixed, weight(index), 1, 1)
    add_small(0, d_in * normed1)
    add_small(1, d_in)
    dimg_ref[0] = (d_resid + norm_back(d_in * vec(0), normed1, rstd1))[0:tokens, :]

    @pl.when(step == last)
    def _():
        big = acc.shape[1]
        g_ref[:, 0:big, :] = acc[...].astype(bf16)
        g_ref[:, big:, :] = jnp.broadcast_to(sacc[...][None], (BLOCKS, SMALL, width)).astype(bf16)


def repack(packed, count, small):
    if packed.shape[0] == count:
        return packed
    have, _, width = packed.shape
    pieces, start = [], 0
    total = packed.shape[1] - SMALL
    old = width // have
    ff_parts = (total - 4 * old) // (2 * old)
    for size in [old] * (4 + ff_parts) + [ff_parts * old]:
        piece = packed[:, start : start + size, :]
        pieces.append(piece.reshape(count, size * have // count, width))
        start += size
    pieces.append(small(packed[:, start:, :]))
    return jnp.concatenate(pieces, axis=1)


def gather_small(block):
    whole = jnp.sum(block.astype(jnp.float32), axis=0, keepdims=True).astype(block.dtype)
    return jnp.concatenate([whole, jnp.zeros((BLOCKS - 1,) + whole.shape[1:], block.dtype)], axis=0)


def run_blocks(alive, images, cotangent, packed):
    count, tokens, width = images.shape
    rows = -(-tokens // 16) * 16
    big = packed.shape[1] - SMALL
    one = lambda i: (i, 0, 0)
    fixed = lambda i: (0, 0, 0)
    return pl.pallas_call(
        functools.partial(block_kernel, count - 1, tokens),
        grid=(count,),
        in_specs=[
            pl.BlockSpec(memory_space=pltpu.SMEM),
            pl.BlockSpec((1, tokens, width), one),
            pl.BlockSpec((1, tokens, width), one),
            pl.BlockSpec(packed.shape, fixed),
        ],
        out_specs=[
            pl.BlockSpec((1, tokens, width), one),
            pl.BlockSpec((1, tokens, width), one),
            pl.BlockSpec(packed.shape, fixed),
        ],
        out_shape=[
            jax.ShapeDtypeStruct(images.shape, jnp.bfloat16),
            jax.ShapeDtypeStruct(images.shape, jnp.float32),
            jax.ShapeDtypeStruct(packed.shape, jnp.bfloat16),
        ],
        scratch_shapes=[
            pltpu.VMEM((rows, width), jnp.float32),
            pltpu.VMEM((rows, width), jnp.float32),
            pltpu.VMEM((BLOCKS, big, width), jnp.float32),
            pltpu.VMEM((SMALL, width), jnp.float32),
            pltpu.VMEM((H, rows, rows), jnp.float32),
            pltpu.VMEM((rows, width), jnp.bfloat16),
            pltpu.VMEM((rows, width), jnp.bfloat16),
            pltpu.VMEM((rows, width), jnp.bfloat16),
            pltpu.VMEM((rows, width), jnp.bfloat16),
        ],
        compiler_params=pltpu.CompilerParams(vmem_limit_bytes=62 * 1024 * 1024),
    )(alive, images, cotangent, packed)


def shards(
    images, cotangent, image_counts, ln1_gain, ln1_bias, qkv_weight, q_bias, v_bias,
    out_weight, out_bias, ln2_gain, ln2_bias, fc1_weight, fc1_bias, fc2_weight, fc2_bias,
):
    micro, slots, tokens, width = images.shape
    shards_count = lax.axis_size("fsdp")
    me = lax.axis_index("fsdp")
    own = ln1_gain.shape[0]
    hidden = fc1_bias.shape[0] * shards_count
    ff_parts = hidden // width
    alive = (jnp.arange(slots)[None, :] < image_counts).astype(jnp.float32).reshape(micro * slots)

    vectors = jnp.stack([ln1_gain, ln1_bias, q_bias, v_bias, out_bias, ln2_gain, ln2_bias, fc2_bias])
    narrow = lax.dynamic_update_slice(jnp.zeros((8, width), jnp.bfloat16), vectors, (0, me * own))
    wide = lax.dynamic_update_slice(jnp.zeros((hidden,), jnp.bfloat16), fc1_bias, (me * fc1_bias.shape[0],))
    wide = wide.reshape(ff_parts, width)
    spare = jnp.zeros((SMALL - 8 - ff_parts, width), jnp.bfloat16)
    cuts = [qkv_weight[:, i * width : (i + 1) * width] for i in range(3)]
    cuts.append(out_weight)
    cuts += [fc1_weight[:, i * width : (i + 1) * width] for i in range(ff_parts)]
    mine = jnp.concatenate(cuts + [fc2_weight, narrow, wide, spare], axis=0)

    gathered = lax.all_gather(mine, "fsdp", axis=0)
    packed = repack(gathered, BLOCKS, gather_small)
    block_out, image_grad, grads = run_blocks(
        alive,
        images.reshape(micro * slots, tokens, width),
        cotangent.reshape(micro * slots, tokens, width),
        packed,
    )
    grads = repack(
        grads,
        shards_count,
        lambda block: jnp.broadcast_to(block[:1], (shards_count,) + block.shape[1:]),
    )
    swapped = lax.all_to_all(grads, "fsdp", 0, 0)
    total = jnp.sum(swapped.astype(jnp.float32), axis=0).astype(jnp.bfloat16)
    copies = lax.all_gather(total, "dp", axis=0)
    total = jnp.sum(copies.astype(jnp.float32), axis=0)

    def cut(index):
        return total[index * own : (index + 1) * own]

    start = (4 + ff_parts) * own
    end = start + fc2_weight.shape[0]
    narrow = lax.dynamic_slice(total[end : end + 8], (0, me * own), (8, own))
    wide = lax.dynamic_slice(
        total[end + 8 : end + 8 + ff_parts].reshape(hidden), (me * fc1_bias.shape[0],), fc1_bias.shape
    )
    return (
        block_out.reshape(images.shape),
        image_grad.reshape(images.shape),
        narrow[0],
        narrow[1],
        jnp.concatenate([cut(i) for i in range(3)], axis=1),
        narrow[2],
        narrow[3],
        cut(3),
        narrow[4],
        narrow[5],
        narrow[6],
        jnp.concatenate([cut(4 + i) for i in range(ff_parts)], axis=1),
        wide,
        total[start:end],
        narrow[7],
    )


def solution(mesh):
    spread = P(None, ("dp", "fsdp"), None, None)
    row = P("fsdp", None)
    one = P("fsdp")
    return jax.shard_map(
        shards,
        mesh=mesh,
        in_specs=(
            spread, spread, P(None, ("dp", "fsdp")), one, one, row, one, one,
            row, one, one, one, row, one, row, one,
        ),
        out_specs=(
            spread, spread, one, one, row, one, one, row, one, one, one, row, one, row, one,
        ),
        check_vma=False,
    )
```

```python
import functools

import jax
import jax.numpy as jnp
from jax import lax
from jax.experimental import pallas as pl
from jax.experimental.pallas import tpu as pltpu
from jax.sharding import PartitionSpec as P

H = 6
HD = 64
LANE = 128
BLOCKS = 8
SMALL = 64
VECTORS = 16
CHUNKS = 5


def dot(left, right, left_dim, right_dim):
    return lax.dot_general(
        left,
        right,
        (((left_dim,), (right_dim,)), ((), ())),
        preferred_element_type=jnp.float32,
    )


def layer_norm(hidden):
    center = hidden - jnp.mean(hidden, axis=-1, keepdims=True)
    rstd = lax.rsqrt(jnp.mean(center * center, axis=-1, keepdims=True) + 1e-06)
    return (center * rstd, rstd)


def norm_back(grad, normed, rstd):
    return rstd * (
        grad
        - jnp.mean(grad, axis=-1, keepdims=True)
        - normed * jnp.mean(grad * normed, axis=-1, keepdims=True)
    )


def block_kernel(
    last, tokens, alive_ref, img_ref, cot_ref, w_ref, out_ref, dimg_ref, g_ref,
    hid, cot, acc, sacc, probs_s, q_s, k_s, v_s, attn_s,
):
    step = pl.program_id(0)
    width = hid.shape[1]
    rows = hid.shape[0]
    part = width // BLOCKS
    ff_parts = (w_ref.shape[1] - SMALL - 4 * part) // (2 * part)
    bf16 = jnp.bfloat16
    f32 = jnp.float32

    @pl.when(step == 0)
    def _():
        hid[...] = jnp.zeros_like(hid)
        cot[...] = jnp.zeros_like(cot)
        acc[...] = jnp.zeros_like(acc)
        sacc[...] = jnp.zeros_like(sacc)

    alive = alive_ref[step]
    hid[0:tokens, :] = img_ref[0].astype(f32)
    cot[0:tokens, :] = cot_ref[0] * alive

    tail = w_ref.shape[1] - SMALL
    small = jnp.sum(w_ref[:, tail : tail + VECTORS, :].astype(f32), axis=0)

    def vec(index):
        return small[index : index + 1, :]

    def weight(index):
        return w_ref[:, index * part : (index + 1) * part, :].reshape(width, width)

    def add(index, value):
        acc[:, index * part : (index + 1) * part, :] += value.reshape(BLOCKS, part, width)

    def fc2(index):
        start = (4 + ff_parts) * part
        chunk = BLOCKS // ff_parts
        return w_ref[index * chunk : (index + 1) * chunk, start : start + ff_parts * part, :].reshape(width, width)

    def add_fc2(index, value):
        start = (4 + ff_parts) * part
        chunk = BLOCKS // ff_parts
        acc[index * chunk : (index + 1) * chunk, start : start + ff_parts * part, :] += value.reshape(
            chunk, ff_parts * part, width
        )

    def add_small(index, value):
        sacc[index : index + 1, :] += jnp.sum(value, axis=0, keepdims=True)

    scale = HD ** (-0.5)
    normed1, rstd1 = layer_norm(hid[...])
    attn_in = (normed1 * vec(0) + vec(1)).astype(bf16)
    q_s[...] = ((dot(attn_in, weight(0), 1, 0) + vec(2)) * scale).astype(bf16)
    k_s[...] = dot(attn_in, weight(1), 1, 0).astype(bf16)
    v_s[...] = (dot(attn_in, weight(2), 1, 0) + vec(3)).astype(bf16)

    low = lax.broadcasted_iota(jnp.int32, (1, LANE), 1) < HD
    masks = (low.astype(f32).astype(bf16), (1.0 - low.astype(f32)).astype(bf16))
    keymask = lax.broadcasted_iota(jnp.int32, (rows, rows), 1) < tokens
    for pair in range(H // 2):
        cols = slice(pair * LANE, (pair + 1) * LANE)
        q, k, v = q_s[:, cols], k_s[:, cols], v_s[:, cols]
        halves = []
        for side in range(2):
            scores = jnp.where(keymask, dot(q * masks[side], k, 1, 1), -1e30)
            expo = jnp.exp(scores - jnp.max(scores, axis=-1, keepdims=True))
            probs = expo * (1.0 / jnp.sum(expo, axis=-1, keepdims=True))
            probs_s[2 * pair + side] = probs
            halves.append(dot(probs.astype(bf16), v, 1, 0))
        attn_s[:, cols] = jnp.where(low, halves[0], halves[1]).astype(bf16)

    attn = attn_s[...]
    resid = hid[...] + dot(attn, weight(3), 1, 0) + vec(4)
    normed2, rstd2 = layer_norm(resid)
    mlp_in = (normed2 * vec(5) + vec(6)).astype(bf16)
    grad_top = cot[...]
    dy = grad_top.astype(bf16)
    add_small(7, grad_top)
    result = resid + vec(7)
    d_mlp = jnp.zeros_like(resid)
    for index in range(ff_parts):
        w_one = weight(4 + index)
        w_two = fc2(index)
        pre = dot(mlp_in, w_one, 1, 0) + vec(8 + index)
        cdf = 0.5 * (1.0 + lax.erf(pre * 0.7071067811865476))
        slope = cdf + pre * jnp.exp(-0.5 * pre * pre) * 0.3989422804014327
        act = (pre * cdf).astype(bf16)
        result = result + dot(act, w_two, 1, 0)
        add_fc2(index, dot(act, dy, 0, 0))
        d_pre = dot(dy, w_two, 1, 1) * slope
        d_pre_b = d_pre.astype(bf16)
        add_small(8 + index, d_pre)
        add(4 + index, dot(mlp_in, d_pre_b, 0, 0))
        d_mlp = d_mlp + dot(d_pre_b, w_one, 1, 1)
    out_ref[0] = (result * alive)[0:tokens, :].astype(bf16)

    add_small(5, d_mlp * normed2)
    add_small(6, d_mlp)
    d_resid = grad_top + norm_back(d_mlp * vec(5), normed2, rstd2)
    d_proj = d_resid.astype(bf16)
    add(3, dot(attn, d_proj, 0, 0))
    add_small(4, d_resid)
    attn_s[...] = dot(d_proj, weight(3), 1, 1).astype(bf16)
    for pair in range(H // 2):
        cols = slice(pair * LANE, (pair + 1) * LANE)
        q, k, v, d_attn = q_s[:, cols], k_s[:, cols], v_s[:, cols], attn_s[:, cols]
        d_q, d_k, d_v = [], [], []
        for side in range(2):
            probs = probs_s[2 * pair + side]
            d_v.append(dot(probs.astype(bf16), d_attn, 0, 0))
            d_probs = dot(d_attn * masks[side], v, 1, 1)
            delta = jnp.sum(probs * d_probs, axis=-1, keepdims=True)
            d_scores = (probs * (d_probs - delta)).astype(bf16)
            d_q.append(dot(d_scores, k, 1, 0))
            d_k.append(dot(d_scores, q, 0, 0))
        d_query = jnp.where(low, d_q[0], d_q[1]) * scale
        d_values = jnp.where(low, d_v[0], d_v[1])
        sacc[2:3, cols] += jnp.sum(d_query, axis=0, keepdims=True)
        sacc[3:4, cols] += jnp.sum(d_values, axis=0, keepdims=True)
        q_s[:, cols] = d_query.astype(bf16)
        k_s[:, cols] = jnp.where(low, d_k[0], d_k[1]).astype(bf16)
        v_s[:, cols] = d_values.astype(bf16)
    d_in = jnp.zeros_like(d_resid)
    for index, piece in enumerate((q_s, k_s, v_s)):
        d_mixed = piece[...]
        add(index, dot(attn_in, d_mixed, 0, 0))
        d_in = d_in + dot(d_mixed, weight(index), 1, 1)
    add_small(0, d_in * normed1)
    add_small(1, d_in)
    dimg_ref[0] = (d_resid + norm_back(d_in * vec(0), normed1, rstd1))[0:tokens, :]

    @pl.when(step == last)
    def _():
        big = acc.shape[1]
        g_ref[:, 0:big, :] = acc[...].astype(bf16)
        g_ref[:, big:, :] = jnp.broadcast_to(sacc[...][None], (BLOCKS, SMALL, width)).astype(bf16)


MESH = pl.DeviceIdType.MESH


def neighbours():
    me = lax.axis_index("fsdp")
    core = lax.rem(me, 2)
    chip = me // 2
    x = lax.rem(chip, 2)
    y = chip // 2
    chips = (chip, y * 2 + 1 - x, (1 - y) * 2 + x, (1 - y) * 2 + 1 - x)
    return me, core, chips


def greet(devices):
    barrier = pltpu.get_barrier_semaphore()
    for device in devices:
        pl.semaphore_signal(barrier, inc=1, device_id=device, device_id_type=MESH)
    pl.semaphore_wait(barrier, len(devices))


def gather_kernel(qkv_ref, proj_ref, one_ref, two_ref, small_ref, out_ref, mine_ref, send_sem, recv_sem):
    me, core, chips = neighbours()
    own, width = proj_ref.shape
    start = 0
    for source in (qkv_ref, proj_ref, one_ref):
        for index in range(source.shape[1] // width):
            mine_ref[start : start + own, :] = source[:, index * width : (index + 1) * width]
            start += own
    mine_ref[start : start + two_ref.shape[0], :] = two_ref[...]
    mine_ref[start + two_ref.shape[0] :, :] = small_ref[...]
    half = mine_ref.shape[0] // 2
    partner = {"fsdp": chips[0] * 2 + 1 - core}
    across = {"fsdp": chips[1] * 2 + core}
    along = {"fsdp": chips[2] * 2 + core}
    greet((partner, across, along))
    started = []

    def slot(chip, side, part):
        return out_ref.at[chips[chip] * 2 + side, pl.ds(part * half, half)]

    def send(index, source, target, device):
        copy = pltpu.make_async_remote_copy(
            src_ref=source, dst_ref=target, send_sem=send_sem.at[index],
            recv_sem=recv_sem.at[index], device_id=device, device_id_type=MESH,
        )
        copy.start()
        started.append(copy)

    def wait(index, target):
        pltpu.make_async_remote_copy(
            src_ref=target, dst_ref=target, send_sem=send_sem.at[index],
            recv_sem=recv_sem.at[index], device_id=partner, device_id_type=MESH,
        ).wait_recv()

    def own(part):
        return mine_ref.at[pl.ds(part * half, half)]

    for step in range(2):
        send(2 + step, own(step), slot(0, core, step), across)
        send(5 - step, own(1 - step), slot(0, core, 1 - step), along)
    for part in range(2):
        send(part, own(part), slot(0, core, part), partner)
    out_ref[me] = mine_ref[...]
    wait(2, slot(1, core, 0))
    send(6, slot(1, core, 0), slot(1, core, 0), along)
    wait(5, slot(2, core, 1))
    send(7, slot(2, core, 1), slot(2, core, 1), across)
    send(8, slot(1, core, 0), slot(1, core, 0), partner)
    send(11, slot(2, core, 1), slot(2, core, 1), partner)
    wait(3, slot(1, core, 1))
    send(9, slot(1, core, 1), slot(1, core, 1), partner)
    wait(4, slot(2, core, 0))
    send(10, slot(2, core, 0), slot(2, core, 0), partner)
    wait(6, slot(3, core, 0))
    send(12, slot(3, core, 0), slot(3, core, 0), partner)
    wait(7, slot(3, core, 1))
    send(13, slot(3, core, 1), slot(3, core, 1), partner)
    for part in range(2):
        wait(part, slot(0, 1 - core, part))
        wait(8 + part, slot(1, 1 - core, part))
        wait(10 + part, slot(2, 1 - core, part))
        wait(12 + part, slot(3, 1 - core, part))
    for copy in started:
        copy.wait_send()


def reduce_kernel(
    groups, g_ref, out_ref, from_partner, summed, from_chips, total, from_groups, quarter_sum, final,
    partner_send, partner_recv, chip_send, chip_recv, group_send, group_recv, back_send, back_recv,
):
    me, core, chips = neighbours()
    group = lax.axis_index("dp")
    rows = g_ref.shape[1]
    chunk = rows // CHUNKS
    piece = chunk // groups
    partner = {"fsdp": chips[0] * 2 + 1 - core}
    peers = [{"fsdp": chips[k] * 2 + core} for k in range(4)]
    others = [lax.rem(group + step, groups) for step in range(1, groups)]
    greet([partner] + peers[1:] + [{"dp": other} for other in others])
    f32, bf16 = jnp.float32, jnp.bfloat16
    started = []

    def copy(source, target, sends, receives, device):
        made = pltpu.make_async_remote_copy(
            src_ref=source, dst_ref=target, send_sem=sends, recv_sem=receives,
            device_id=device, device_id_type=MESH,
        )
        made.start()
        started.append(made)

    def wait(target, sends, receives):
        pltpu.make_async_remote_copy(
            src_ref=target, dst_ref=target, send_sem=sends, recv_sem=receives,
            device_id=partner, device_id_type=MESH,
        ).wait_recv()

    def span(c):
        return pl.ds(c * chunk, chunk)

    def quarter(c, owner):
        return pl.ds(pl.multiple_of(c * chunk + owner * piece, piece), piece)

    order = (3, 1, 2, 0)
    for c in range(CHUNKS):
        for k in order:
            copy(
                g_ref.at[chips[k] * 2 + 1 - core, span(c)], from_partner.at[k, span(c)],
                partner_send.at[c, k], partner_recv.at[c, k], partner,
            )
    for c in range(CHUNKS):
        for k in order:
            wait(from_partner.at[k, span(c)], partner_send.at[c, k], partner_recv.at[c, k])
            both = g_ref[chips[k] * 2 + core, span(c)].astype(f32) + from_partner[k, span(c)].astype(f32)
            summed[k, span(c)] = both.astype(bf16)
            if k:
                copy(
                    summed.at[k, span(c)], from_chips.at[k - 1, span(c)],
                    chip_send.at[c, k], chip_recv.at[c, k], peers[k],
                )
    for c in range(CHUNKS):
        whole = summed[0, span(c)].astype(f32)
        for k in (1, 2, 3):
            wait(from_chips.at[k - 1, span(c)], chip_send.at[c, k], chip_recv.at[c, k])
            whole = whole + from_chips[k - 1, span(c)].astype(f32)
        total[span(c)] = whole.astype(bf16)
        for step, other in enumerate(others):
            copy(
                total.at[quarter(c, other)], from_groups.at[c, step],
                group_send.at[c, step], group_recv.at[c, step], {"dp": other},
            )
    for c in range(CHUNKS):
        whole = total[quarter(c, group)].astype(f32)
        for step in range(groups - 1):
            wait(from_groups.at[c, step], group_send.at[c, step], group_recv.at[c, step])
            whole = whole + from_groups[c, step].astype(f32)
        quarter_sum[c] = whole.astype(bf16)
        final[quarter(c, group)] = whole.astype(bf16)
        for step, other in enumerate(others):
            copy(
                quarter_sum.at[c], final.at[quarter(c, group)],
                back_send.at[c, step], back_recv.at[c, step], {"dp": other},
            )
    for c in range(CHUNKS):
        for step in range(groups - 1):
            source = lax.rem(group + groups - 1 - step, groups)
            wait(final.at[quarter(c, source)], back_send.at[c, step], back_recv.at[c, step])
    out_ref[...] = final[...].astype(f32)
    for made in started:
        made.wait_send()


def gather_shards(qkv, proj, one, two, small):
    width = proj.shape[1]
    rows = (qkv.size + proj.size + one.size + two.size + small.size) // width
    return pl.pallas_call(
        gather_kernel,
        out_shape=jax.ShapeDtypeStruct((BLOCKS, rows, width), jnp.bfloat16),
        in_specs=[pl.BlockSpec(memory_space=pltpu.VMEM)] * 5,
        out_specs=pl.BlockSpec(memory_space=pltpu.VMEM),
        scratch_shapes=[pltpu.VMEM((rows, width), jnp.bfloat16), pltpu.SemaphoreType.DMA((14,)), pltpu.SemaphoreType.DMA((14,))],
        compiler_params=pltpu.CompilerParams(collective_id=0, has_side_effects=True),
    )(qkv, proj, one, two, small)


def reduce_shards(grads, groups):
    _, rows, width = grads.shape
    bf16 = jnp.bfloat16
    piece = rows // CHUNKS // groups
    dma = pltpu.SemaphoreType.DMA
    return pl.pallas_call(
        functools.partial(reduce_kernel, groups),
        out_shape=jax.ShapeDtypeStruct((rows, width), jnp.float32),
        in_specs=[pl.BlockSpec(memory_space=pltpu.VMEM)],
        out_specs=pl.BlockSpec(memory_space=pltpu.VMEM),
        scratch_shapes=[
            pltpu.VMEM((4, rows, width), bf16),
            pltpu.VMEM((4, rows, width), bf16),
            pltpu.VMEM((3, rows, width), bf16),
            pltpu.VMEM((rows, width), bf16),
            pltpu.VMEM((CHUNKS, groups - 1, piece, width), bf16),
            pltpu.VMEM((CHUNKS, piece, width), bf16),
            pltpu.VMEM((rows, width), bf16),
        ]
        + [dma((CHUNKS, 4))] * 4
        + [dma((CHUNKS, groups - 1))] * 4,
        compiler_params=pltpu.CompilerParams(collective_id=1, has_side_effects=True),
    )(grads)


def repack(packed, count, small):
    if packed.shape[0] == count:
        return packed
    have, _, width = packed.shape
    pieces, start = [], 0
    total = packed.shape[1] - SMALL
    old = width // have
    ff_parts = (total - 4 * old) // (2 * old)
    for size in [old] * (4 + ff_parts) + [ff_parts * old]:
        piece = packed[:, start : start + size, :]
        pieces.append(piece.reshape(count, size * have // count, width))
        start += size
    pieces.append(small(packed[:, start:, :]))
    return jnp.concatenate(pieces, axis=1)


def gather_small(block):
    whole = jnp.sum(block.astype(jnp.float32), axis=0, keepdims=True).astype(block.dtype)
    return jnp.concatenate([whole, jnp.zeros((BLOCKS - 1,) + whole.shape[1:], block.dtype)], axis=0)


def run_blocks(alive, images, cotangent, packed):
    count, tokens, width = images.shape
    rows = -(-tokens // 16) * 16
    big = packed.shape[1] - SMALL
    one = lambda i: (i, 0, 0)
    fixed = lambda i: (0, 0, 0)
    return pl.pallas_call(
        functools.partial(block_kernel, count - 1, tokens),
        grid=(count,),
        in_specs=[
            pl.BlockSpec(memory_space=pltpu.SMEM),
            pl.BlockSpec((1, tokens, width), one),
            pl.BlockSpec((1, tokens, width), one),
            pl.BlockSpec(packed.shape, fixed),
        ],
        out_specs=[
            pl.BlockSpec((1, tokens, width), one),
            pl.BlockSpec((1, tokens, width), one),
            pl.BlockSpec(packed.shape, fixed),
        ],
        out_shape=[
            jax.ShapeDtypeStruct(images.shape, jnp.bfloat16),
            jax.ShapeDtypeStruct(images.shape, jnp.float32),
            jax.ShapeDtypeStruct(packed.shape, jnp.bfloat16),
        ],
        scratch_shapes=[
            pltpu.VMEM((rows, width), jnp.float32),
            pltpu.VMEM((rows, width), jnp.float32),
            pltpu.VMEM((BLOCKS, big, width), jnp.float32),
            pltpu.VMEM((SMALL, width), jnp.float32),
            pltpu.VMEM((H, rows, rows), jnp.float32),
            pltpu.VMEM((rows, width), jnp.bfloat16),
            pltpu.VMEM((rows, width), jnp.bfloat16),
            pltpu.VMEM((rows, width), jnp.bfloat16),
            pltpu.VMEM((rows, width), jnp.bfloat16),
        ],
        compiler_params=pltpu.CompilerParams(vmem_limit_bytes=62 * 1024 * 1024),
    )(alive, images, cotangent, packed)


def shards(
    images, cotangent, image_counts, ln1_gain, ln1_bias, qkv_weight, q_bias, v_bias,
    out_weight, out_bias, ln2_gain, ln2_bias, fc1_weight, fc1_bias, fc2_weight, fc2_bias,
):
    micro, slots, tokens, width = images.shape
    shards_count = lax.axis_size("fsdp")
    me = lax.axis_index("fsdp")
    own = ln1_gain.shape[0]
    hidden = fc1_bias.shape[0] * shards_count
    ff_parts = hidden // width
    alive = (jnp.arange(slots)[None, :] < image_counts).astype(jnp.float32).reshape(micro * slots)

    vectors = jnp.stack([ln1_gain, ln1_bias, q_bias, v_bias, out_bias, ln2_gain, ln2_bias, fc2_bias])
    narrow = lax.dynamic_update_slice(jnp.zeros((8, width), jnp.bfloat16), vectors, (0, me * own))
    wide = lax.dynamic_update_slice(jnp.zeros((hidden,), jnp.bfloat16), fc1_bias, (me * fc1_bias.shape[0],))
    wide = wide.reshape(ff_parts, width)
    spare = jnp.zeros((SMALL - 8 - ff_parts, width), jnp.bfloat16)
    small = jnp.concatenate([narrow, wide, spare], axis=0)
    groups = lax.axis_size("dp")
    direct = shards_count == BLOCKS
    if direct:
        packed = gather_shards(qkv_weight, out_weight, fc1_weight, fc2_weight, small)
    else:
        cuts = [qkv_weight[:, i * width : (i + 1) * width] for i in range(3)]
        cuts.append(out_weight)
        cuts += [fc1_weight[:, i * width : (i + 1) * width] for i in range(ff_parts)]
        mine = jnp.concatenate(cuts + [fc2_weight, small], axis=0)
        packed = repack(lax.all_gather(mine, "fsdp", axis=0), BLOCKS, gather_small)
    block_out, image_grad, grads = run_blocks(
        alive,
        images.reshape(micro * slots, tokens, width),
        cotangent.reshape(micro * slots, tokens, width),
        packed,
    )
    if direct:
        total = reduce_shards(grads, groups)
    else:
        grads = repack(
            grads,
            shards_count,
            lambda block: jnp.broadcast_to(block[:1], (shards_count,) + block.shape[1:]),
        )
        swapped = lax.all_to_all(grads, "fsdp", 0, 0)
        total = jnp.sum(swapped.astype(jnp.float32), axis=0).astype(jnp.bfloat16)
        total = jnp.sum(lax.all_gather(total, "dp", axis=0).astype(jnp.float32), axis=0)

    def cut(index):
        return total[index * own : (index + 1) * own]

    start = (4 + ff_parts) * own
    end = start + fc2_weight.shape[0]
    narrow = lax.dynamic_slice(total[end : end + 8], (0, me * own), (8, own))
    wide = lax.dynamic_slice(
        total[end + 8 : end + 8 + ff_parts].reshape(hidden), (me * fc1_bias.shape[0],), fc1_bias.shape
    )
    return (
        block_out.reshape(images.shape),
        image_grad.reshape(images.shape),
        narrow[0],
        narrow[1],
        jnp.concatenate([cut(i) for i in range(3)], axis=1),
        narrow[2],
        narrow[3],
        cut(3),
        narrow[4],
        narrow[5],
        narrow[6],
        jnp.concatenate([cut(4 + i) for i in range(ff_parts)], axis=1),
        wide,
        total[start:end],
        narrow[7],
    )


def solution(mesh):
    spread = P(None, ("dp", "fsdp"), None, None)
    row = P("fsdp", None)
    one = P("fsdp")
    return jax.shard_map(
        shards,
        mesh=mesh,
        in_specs=(
            spread, spread, P(None, ("dp", "fsdp")), one, one, row, one, one,
            row, one, one, one, row, one, row, one,
        ),
        out_specs=(
            spread, spread, one, one, row, one, one, row, one, one, one, row, one, row, one,
        ),
        check_vma=False,
    )
```
